256 devices in a mesh: ctx: 8 (over z_hi, y), tp: 32 (over z_lo, x, core).
Axes of the slice: x: 4, y: 4, z: 8 (z_hi: 2, z_lo: 4; z = z_hi * 4 + z_lo), core: 2. Of those that a mesh axis runs over, the one named last changes fastest.
Arguments:
- streams: bfloat16 [3, 1, 3072, 8192], P(None, None, 'ctx', 'tp'), may hold values from -6 to 6
- taps: float32 [3, 7, 8192], P(None, None, 'tp'), may hold values from -2.4 to 2.4
- decay: float32 [16, 8192], P(None, 'tp'), may hold values from 0.96 to 1, as said below
- residues: float32 [16, 8192], P(None, 'tp'), may hold values from -0.12 to 0.12
- init_state: float32 [1, 16, 8192], P(None, None, 'tp'), may hold values from -48 to 48
- out_weight: bfloat16 [8192, 8192], P('tp'), may hold values from -0.125 to 0.125
Outputs:
- mixed: bfloat16 [1, 3072, 8192], P(None, 'ctx', 'tp')
The draws below stay inside these ranges and needn't reach their ends.
Inputs may be any that keep to these rules, and one draw needn't show every extreme that they name: `decay`: each pole's factor lies strictly between 0 and 1.
All inputs are finite; a program needn't handle non-finite values.
Results may differ from the reference program's by a relative error of at most 0.0049.
Values may be sent and summed in bfloat16 or wider, within the bound.
A program may use at most 128 MiB of HBM per device.

```python
import jax
import jax.numpy as jnp
from jax import lax

D = 8192
POLES = 16
TAPS = 7
SEQS = 1
WINDOW = 3072


def draw_decay(key, part):
    key_pick, key_slow, key_fast = jax.random.split(jax.random.fold_in(key, 11), 3)
    slow_share = 0.5
    picked = jax.random.uniform(key_pick, (POLES, D), jnp.float32) < slow_share
    slow_rate = jnp.exp(jax.random.uniform(key_slow, (POLES, D), jnp.float32, jnp.log(0.1 / WINDOW), jnp.log(2.0 / WINDOW)))
    fast_rate = jnp.exp(jax.random.uniform(key_fast, (POLES, D), jnp.float32, jnp.log(1.0 / 50.0), jnp.log(1.0 / 30.0)))
    rate = jnp.minimum(jnp.where(picked, slow_rate, fast_rate), 1.0 / 30.0)
    return jnp.exp(-rate).astype(jnp.float32)


def spiked(entries, rng, source, target, blocks, factor):
    owner, partner = [(jnp.arange(entries.shape[position]) // (entries.shape[position] // blocks)).reshape([-1 if axis == position else 1 for axis in range(entries.ndim)]) for position in (source, target)]
    chosen = jax.random.permutation(rng, blocks)[partner]
    strong = (owner == chosen) | (owner == (partner + blocks // 2) % blocks)
    return jnp.where(strong, factor * entries, entries)


def shard_levels(key, dims, cuts, smallest, top_value):
    level, own = 1.0, jax.random.fold_in(key, 6)
    for axis_at, shards_of in cuts:
        steps = jnp.exp(jax.random.uniform(jax.random.fold_in(own, axis_at), (shards_of,), jnp.float32, smallest / len(cuts), top_value / len(cuts)))
        level = level * jnp.repeat(steps, dims[axis_at] // shards_of).reshape([-1 if axis == axis_at else 1 for axis in range(len(dims))])
    return level


def gaussian(key, extent, width, reach, shards=(), kind=jnp.bfloat16):
    result = width * jax.random.normal(key, extent, jnp.float32)
    if shards:
        result = result * shard_levels(key, extent, shards, -0.22, 0.18)
    return jnp.clip(result, -reach, reach).astype(kind)


def heavy_noise(key, shape, width, limit, cuts, heavy, held_as=jnp.bfloat16):
    values = width * jax.random.normal(key, shape, jnp.float32)
    if cuts:
        values = values * shard_levels(key, shape, cuts, -0.22, 0.18)
    return jnp.clip(spiked(values, jax.random.fold_in(key, 3), *heavy), -limit, limit).astype(held_as)


def setup_inputs(seed: int = 0) -> dict:
    streams_of = jax.random.split(jax.random.key(seed), 7)
    return {
        "streams": gaussian(streams_of[0], (3, SEQS, WINDOW, D), 1.0, 6.0, ((2, 8), (3, 32))),
        "taps": gaussian(streams_of[1], (3, TAPS, D), 0.4, 2.4, ((2, 32),), jnp.float32),
        "decay": draw_decay(jax.random.fold_in(streams_of[6], 71), 0),
        "residues": gaussian(streams_of[3], (POLES, D), 0.02, 0.12, ((1, 32),), jnp.float32),
        "init_state": gaussian(streams_of[4], (SEQS, POLES, D), 8.0, 48.0, ((2, 32),), jnp.float32),
        "out_weight": heavy_noise(streams_of[5], (D, D), D ** -0.5, 0.125, ((0, 32),), (0, 1, 32, 2.75)),
    }


def reference(streams, taps, decay, residues, init_state, out_weight):
    tap_lag = TAPS - 1
    widened = jnp.pad(streams.astype(jnp.float32), ((0, 0), (0, 0), (tap_lag, 0), (0, 0)))
    featured = jnp.zeros(streams.shape, jnp.float32)
    for tap_index in range(TAPS):
        featured = featured + taps[:, tap_index][:, None, None, :] * widened[:, :, tap_lag - tap_index:tap_lag - tap_index + WINDOW, :]
    queries = featured[0]
    driven = featured[1] * featured[2]

    def advance(running, driven_now):
        running = decay[None] * running + driven_now[:, None, :]
        return running, jnp.sum(residues[None] * running, axis=1)

    _, outputs = lax.scan(advance, init_state, jnp.swapaxes(driven, 0, 1))
    response = jnp.swapaxes(outputs, 0, 1)
    gated_out = (queries * response).astype(jnp.bfloat16)
    mixed = jnp.dot(gated_out.reshape(SEQS * WINDOW, D), out_weight, preferred_element_type=jnp.float32)
    return mixed.astype(jnp.bfloat16).reshape(SEQS, WINDOW, D)
```

```python
import jax
import jax.numpy as jnp
from jax import lax
from jax.experimental import pallas as pl
from jax.experimental.pallas import tpu as pltpu
from jax.sharding import PartitionSpec as P

MESH = pl.DeviceIdType.MESH
F32 = jnp.float32
BF16 = jnp.bfloat16

NX, NZ, NY, NH = 4, 4, 4, 2
SUB = 8
LANES = 128
HALO = 16


def order_of(z, k):
    if k == 0:
        return jnp.where(z < 2, 3, 0)
    if k == 1:
        return jnp.where(z == 0, 2, jnp.where(z == 1, 0, jnp.where(z == 2, 3, 1)))
    if k == 2:
        return jnp.where(z % 2 == 0, 1, 2)
    return z


def kernel(
    streams, taps, decay, residues, init, weight, out,
    xbf, halo, xs, q_s, d_s, r_s, tapb, decb, resb, lst, ent, ebuf, tbuf, own_e,
    w_own, w_far, gat, pbuf, sendbuf, rbuf, pfin,
    load_sem, wload_sem, halo_sem, e_ssem, e_rsem, t_sem,
    wp_ssem, wp_rsem, wd_ssem, wd_rsem, f1_ssem, f1_rsem, f2_ssem, f2_rsem,
    g_ssem, g_rsem, gp_ssem, gp_rsem, z_ssem, z_rsem,
):
    tp, ctx = lax.axis_index("tp"), lax.axis_index("ctx")
    core, x, z = tp % 2, (tp // 2) % NX, tp // (2 * NX)
    y, zh = ctx % NY, ctx // NY
    nctx = NY * NH
    length = streams.shape[2]
    chans = streams.shape[3]
    poles = decay.shape[0]
    tap_count = taps.shape[1]
    lag = tap_count - 1
    sub_len = length // SUB
    half = length // 2
    groups = chans // LANES
    quarter = chans // NY

    def tp_of(zi, xi, ci):
        return (zi * NX + xi) * 2 + ci

    def dev(tp_index=tp, ctx_index=ctx):
        return {"ctx": ctx_index, "tp": tp_index}

    def remote(src, dst, ssem, rsem, where):
        return pltpu.make_async_remote_copy(
            src_ref=src, dst_ref=dst, send_sem=ssem, recv_sem=rsem, device_id=where, device_id_type=MESH
        )

    def ctx_of(hi, yi):
        return hi * NY + yi

    partner = dev(tp_of(z, x, 1 - core))
    xp, xm = (x + 1) % NX, (x + NX - 1) % NX
    yp, ym = (y + 1) % NY, (y + NY - 1) % NY
    ctx_next, ctx_prev = (ctx + 1) % nctx, (ctx + nctx - 1) % nctx

    barrier = pltpu.get_barrier_semaphore()
    greeted = [partner, dev(tp_of((z + 1) % NZ, x, core)), dev(tp_of((z + NZ - 1) % NZ, x, core))]
    for dx in range(1, NX):
        for dc in range(2):
            greeted.append(dev(tp_of(z, (x + dx) % NX, (core + dc) % 2)))
    for dy in range(1, NY):
        greeted.append(dev(tp, ctx_of(zh, (y + dy) % NY)))
    greeted += [dev(tp, ctx_next), dev(tp, ctx_prev), dev(tp, ctx_of(1 - zh, y))]
    for where in greeted:
        pl.semaphore_signal(barrier, inc=1, device_id=where, device_id_type=MESH)

    load = pltpu.make_async_copy(streams.at[:, 0], xbf, load_sem)
    load.start()

    def w_cols(zt, xi, ci):
        return pl.ds(pl.multiple_of(tp_of(zt, xi, ci) * chans, chans), chans)

    own_loads = []
    for k in range(NZ):
        zt = order_of(z, k)
        own_loads.append(
            pltpu.make_async_copy(weight.at[:, w_cols(zt, x, core)], w_own.at[k, pl.ds(0, chans)], wload_sem.at[k])
        )
    load.wait()

    for g in range(groups):
        lanes = slice(g * LANES, (g + 1) * LANES)
        for s in range(3):
            for i in range(tap_count):
                tapb[g, s * tap_count + i] = jnp.broadcast_to(taps[s, i : i + 1, lanes], (SUB, LANES))
        for n in range(poles):
            decb[g, n] = jnp.broadcast_to(decay[n : n + 1, lanes], (SUB, LANES))
            resb[g, n] = jnp.broadcast_to(residues[n : n + 1, lanes], (SUB, LANES))
        for s in range(3):
            xs[s * groups + g, pl.ds(HALO, length), :] = xbf[s, :, lanes].astype(F32)

    def featurize(first, last):
        for g in range(groups):
            def one(j, carry, g=g):
                feats = []
                for s in range(3):
                    total = None
                    for i in range(tap_count):
                        rows = xs[s * groups + g, pl.ds(HALO + j - i, SUB, stride=sub_len), :]
                        term = tapb[g, s * tap_count + i] * rows
                        total = term if total is None else total + term
                    feats.append(total)
                q_s[g, j] = feats[0]
                d_s[g, j] = feats[1] * feats[2]
                return carry

            lax.fori_loop(first, last, one, 0, unroll=2)

    featurize(lag, sub_len)

    pl.semaphore_wait(barrier, len(greeted))

    halo_copy = remote(
        streams.at[:, 0, pl.ds(length - HALO, HALO)], halo, halo_sem.at[0], halo_sem.at[1], dev(tp, ctx_next)
    )

    @pl.when(ctx < nctx - 1)
    def _():
        halo_copy.start()

    wp_copies, wd_copies = [], []
    for k in range(NZ):
        zt = order_of(z, k)
        own_loads[k].start()
        copy = remote(
            weight.at[:, w_cols(zt, x, 1 - core)], w_own.at[k, pl.ds(chans, chans)], wp_ssem.at[k], wp_rsem.at[k], partner
        )
        copy.start()
        wp_copies.append(copy)
        rows = pl.ds(pl.multiple_of(y * quarter, quarter), quarter)
        sends = []
        for dx in (1, 3, 2):
            for dc in range(2):
                xi, ci = (x + dx) % NX, (core + dc) % 2
                slot = (NX - dx) * 2 + dc - 2
                copy = remote(
                    weight.at[rows, w_cols(zt, xi, ci)],
                    w_far.at[k, y, pl.ds(slot * quarter, quarter)],
                    wd_ssem.at[k, slot], wd_rsem.at[k, slot], dev(tp_of(z, xi, ci)),
                )
                copy.start()
                sends.append(copy)
        wd_copies.append(sends)

    far_rows = w_far.shape[2]
    y_next, y_prev = dev(tp, ctx_of(zh, yp)), dev(tp, ctx_of(zh, ym))
    y_opp = (y + 2) % NY
    f1 = [
        [
            remote(w_far.at[k, y], w_far.at[k, y], f1_ssem.at[k, d], f1_rsem.at[k, d], where)
            for d, where in enumerate((y_next, y_prev))
        ]
        for k in range(NZ)
    ]
    top, bottom = pl.ds(0, far_rows // 2), pl.ds(far_rows // 2, far_rows // 2)
    f2 = [
        [
            remote(w_far.at[k, ym, top], w_far.at[k, ym, top], f2_ssem.at[k, 0], f2_rsem.at[k, 0], y_next),
            remote(w_far.at[k, yp, bottom], w_far.at[k, yp, bottom], f2_ssem.at[k, 1], f2_rsem.at[k, 1], y_prev),
        ]
        for k in range(NZ)
    ]

    def forward_once(k):
        for copy in wd_copies[k]:
            copy.wait_recv()
        for copy in f1[k]:
            copy.start()

    def forward_twice(k):
        for copy in f1[k]:
            copy.wait_recv()
        for copy in f2[k]:
            copy.start()

    @pl.when(ctx > 0)
    def _():
        halo_copy.wait_recv()
        for g in range(groups):
            for s in range(3):
                xs[s * groups + g, pl.ds(0, HALO), :] = halo[s, :, g * LANES : (g + 1) * LANES].astype(F32)

    @pl.when(ctx == 0)
    def _():
        for g in range(groups):
            for s in range(3):
                xs[s * groups + g, pl.ds(0, HALO), :] = jnp.zeros((HALO, LANES), F32)

    featurize(0, lag)

    for g in range(groups):
        def step(j, states, g=g):
            driven = d_s[g, j]
            new = tuple(decb[g, n] * states[n] + driven for n in range(poles))
            parts = [resb[g, n] * new[n] for n in range(poles)]
            while len(parts) > 1:
                parts = [a + b for a, b in zip(parts[::2], parts[1::2])]
            r_s[g, j] = parts[0]
            return new

        states = lax.fori_loop(0, sub_len, step, tuple(jnp.zeros((SUB, LANES), F32) for _ in range(poles)), unroll=2)
        for n in range(poles):
            lst[g, pl.ds(n * SUB, SUB), :] = states[n]

    def power(value, count):
        result, base = None, value
        while count:
            if count % 2:
                result = base if result is None else result * base
            count //= 2
            if count:
                base = base * base
        return result

    for g in range(groups):
        lanes = slice(g * LANES, (g + 1) * LANES)
        sub_decay = power(decay[:, lanes], sub_len)
        running = jnp.zeros((poles, LANES), F32)
        for s in range(SUB):
            ent[g, s] = running
            running = sub_decay * running + lst[g, pl.ds(s, poles, stride=SUB), :]
        own_e[:, lanes] = running

    e_copies = [
        remote(own_e, ebuf.at[dy - 1], e_ssem.at[dy - 1], e_rsem.at[dy - 1], dev(tp, ctx_of(zh, (y + dy) % NY)))
        for dy in range(1, NY)
    ]
    for copy in e_copies:
        copy.start()

    forward_once(0)

    for copy in e_copies:
        copy.wait_recv()

    def select_power(powers, exponent):
        value = jnp.broadcast_to(jnp.where(exponent == 0, F32(1.0), F32(0.0)), powers[0].shape)
        for e, p in enumerate(powers):
            value = jnp.where(exponent == e + 1, p, value)
        return value

    t_copy = remote(tbuf.at[0], tbuf.at[1], t_sem.at[0], t_sem.at[1], dev(tp, ctx_of(1 - zh, y)))

    shard_decay = power(decay[...], length)
    powers = [shard_decay, shard_decay * shard_decay]
    powers.append(powers[1] * shard_decay)

    @pl.when(zh == 0)
    def _():
        total = powers[2] * shard_decay * init[0] + select_power(powers, 3 - y) * own_e[...]
        for dy in range(1, NY):
            total = total + select_power(powers, 3 - (y + NY - dy) % NY) * ebuf[dy - 1]
        tbuf[0] = total
        t_copy.start()
        tbuf[2] = init[0]

    @pl.when(zh == 1)
    def _():
        t_copy.wait_recv()
        tbuf[2] = tbuf[1]

    incoming = select_power(powers, y) * tbuf[2]
    for dy in range(1, NY):
        gain = F32(1.0) if dy == 1 else powers[dy - 2]
        incoming = incoming + jnp.where(y >= dy, gain * ebuf[dy - 1], F32(0.0))

    for g in range(groups):
        lanes = slice(g * LANES, (g + 1) * LANES)
        sub_decay = power(decay[:, lanes], sub_len)
        arriving = incoming[:, lanes]
        for s in range(SUB):
            lst[g, pl.ds(s, poles, stride=SUB), :] = (ent[g, s] + arriving) * residues[:, lanes]
            arriving = arriving * sub_decay

    for g in range(groups):
        states = tuple(lst[g, pl.ds(n * SUB, SUB), :] for n in range(poles))
        for h in range(2):
            def pair(jj, states, g=g, h=h):
                rows = []
                for b in range(2):
                    j = h * (sub_len // 2) + 2 * jj + b
                    states = tuple(decb[g, n] * states[n] for n in range(poles))
                    parts = list(states)
                    while len(parts) > 1:
                        parts = [u + v for u, v in zip(parts[::2], parts[1::2])]
                    rows.append(q_s[g, j] * (r_s[g, j] + parts[0]))
                at = pl.ds(pl.multiple_of(jj * 2 * SUB, 2 * SUB), 2 * SUB)
                gat[h, at, g * LANES : (g + 1) * LANES] = jnp.concatenate(rows, axis=0).astype(BF16)
                return states

            states = lax.fori_loop(0, sub_len // 4, pair, states)

    def block(h, slot):
        return gat.at[h, :, pl.ds(slot * chans, chans)]

    def g_copy(h, src_slot, dst_slot, at, where):
        return remote(block(h, src_slot), block(h, dst_slot), g_ssem.at[at], g_rsem.at[at], where)

    def p_copy(h, slot):
        return remote(
            block(h, slot), block(h, slot + 1), gp_ssem.at[h, slot // 2], gp_rsem.at[h, slot // 2], partner
        )

    to_right, to_left = dev(tp_of(z, xp, core)), dev(tp_of(z, xm, core))
    right = [g_copy(0, 0, 6, 0, to_right), g_copy(1, 0, 6, 1, to_right)]
    left = [g_copy(0, 0, 2, 2, to_left), g_copy(1, 0, 2, 3, to_left)]
    relay_right = g_copy(0, 6, 4, 4, to_right)
    relay_left = g_copy(1, 2, 4, 5, to_left)
    right[0].start()
    left[1].start()
    right[1].start()
    left[0].start()
    p_copies = [[p_copy(h, slot) for slot in (0, 2, 4, 6)] for h in range(2)]
    for h in range(2):
        p_copies[h][0].start()

    forward_once(1)
    right[0].wait_recv()
    relay_right.start()
    p_copies[0][3].start()
    left[1].wait_recv()
    relay_left.start()
    p_copies[1][1].start()
    right[1].wait_recv()
    p_copies[1][3].start()
    left[0].wait_recv()
    p_copies[0][1].start()
    forward_twice(0)
    forward_once(2)
    relay_right.wait_recv()
    p_copies[0][2].start()
    relay_left.wait_recv()
    p_copies[1][2].start()
    forward_twice(1)
    for h in range(2):
        for copy in p_copies[h]:
            copy.wait_recv()

    z_copies = []
    for k in range(NZ):
        if k == 1:
            forward_once(3)
            forward_twice(2)
        if k == 2:
            forward_twice(3)
        zt = order_of(z, k)
        own_loads[k].wait()
        wp_copies[k].wait_recv()
        for copy in f2[k]:
            copy.wait_recv()
        pieces = [w_own[k]]
        for slot in range(2 * NX - 2):
            for q in range(NY):
                pieces.append(w_far[k, q, slot * quarter : (slot + 1) * quarter])
        w_all = jnp.concatenate(pieces, axis=0)
        for h in range(2):
            product = jnp.dot(gat[h], w_all, preferred_element_type=F32)
            if k < NZ - 1:
                heading = jnp.where(zt > z, 0, 1)
                target = jnp.where(zt > z, z + 1, z - 1)
                copy = remote(
                    sendbuf.at[k, h], rbuf.at[heading, zt, h], z_ssem.at[k, h], z_rsem.at[heading, zt, h],
                    dev(tp_of(target, x, core)),
                )
                pbuf[...] = product
                has_in = jnp.where(zt > z, z > 0, z < NZ - 1)

                @pl.when(has_in)
                def _(copy=copy, heading=heading, zt=zt, h=h):
                    copy.wait_recv()
                    pbuf[...] += rbuf[heading, zt, h].astype(F32)

                sendbuf[k, h] = pbuf[...].astype(BF16)
                copy.start()
                z_copies.append(copy)
            else:
                pbuf[...] = product

                @pl.when(z > 0)
                def _(h=h):
                    remote(
                        sendbuf.at[0, h], rbuf.at[0, z, h], z_ssem.at[0, h], z_rsem.at[0, z, h], partner
                    ).wait_recv()
                    pbuf[...] += rbuf[0, z, h].astype(F32)

                @pl.when(z < NZ - 1)
                def _(h=h):
                    remote(
                        sendbuf.at[0, h], rbuf.at[1, z, h], z_ssem.at[0, h], z_rsem.at[1, z, h], partner
                    ).wait_recv()
                    pbuf[...] += rbuf[1, z, h].astype(F32)

                for g in range(groups):
                    pfin[g, pl.ds(h * half, half), :] = pbuf[:, g * LANES : (g + 1) * LANES]

    for g in range(groups):
        for s in range(SUB):
            out[0, s * sub_len : (s + 1) * sub_len, g * LANES : (g + 1) * LANES] = pfin[
                g, pl.ds(s, sub_len, stride=SUB), :
            ].astype(BF16)

    @pl.when(ctx < nctx - 1)
    def _():
        halo_copy.wait_send()

    @pl.when(zh == 0)
    def _():
        t_copy.wait_send()

    sent = e_copies + wp_copies + right + left + [relay_right, relay_left] + z_copies
    for k in range(NZ):
        sent = sent + wd_copies[k] + f1[k] + f2[k]
    for h in range(2):
        sent = sent + p_copies[h]
    for copy in sent:
        copy.wait_send()


def per_device(streams, taps, decay, residues, init_state, out_weight):
    length, chans = streams.shape[2], streams.shape[3]
    poles, tap_count = decay.shape[0], taps.shape[1]
    groups, sub_len, half, quarter = chans // LANES, length // SUB, length // 2, chans // NY
    vmem = pl.BlockSpec(memory_space=pltpu.VMEM)
    hbm = pl.BlockSpec(memory_space=pl.ANY)
    dma = pltpu.SemaphoreType.DMA
    return pl.pallas_call(
        kernel,
        out_shape=jax.ShapeDtypeStruct((1, length, chans), BF16),
        in_specs=[hbm, vmem, vmem, vmem, vmem, hbm],
        out_specs=vmem,
        scratch_shapes=[
            pltpu.VMEM((3, length, chans), BF16),
            pltpu.VMEM((3, HALO, chans), BF16),
            pltpu.VMEM((3 * groups, HALO + length, LANES), F32),
            pltpu.VMEM((groups, sub_len, SUB, LANES), F32),
            pltpu.VMEM((groups, sub_len, SUB, LANES), F32),
            pltpu.VMEM((groups, sub_len, SUB, LANES), F32),
            pltpu.VMEM((groups, 3 * tap_count, SUB, LANES), F32),
            pltpu.VMEM((groups, poles, SUB, LANES), F32),
            pltpu.VMEM((groups, poles, SUB, LANES), F32),
            pltpu.VMEM((groups, poles * SUB, LANES), F32),
            pltpu.VMEM((groups, SUB, poles, LANES), F32),
            pltpu.VMEM((NY - 1, poles, chans), F32),
            pltpu.VMEM((3, poles, chans), F32),
            pltpu.VMEM((poles, chans), F32),
            pltpu.VMEM((NZ, 2 * chans, chans), BF16),
            pltpu.VMEM((NZ, NY, (2 * NX - 2) * quarter, chans), BF16),
            pltpu.VMEM((2, half, 2 * NX * chans), BF16),
            pltpu.VMEM((half, chans), F32),
            pltpu.VMEM((NZ - 1, 2, half, chans), BF16),
            pltpu.VMEM((2, NZ, 2, half, chans), BF16),
            pltpu.VMEM((groups, length, LANES), F32),
            dma(()), dma((NZ,)), dma((2,)), dma((NY - 1,)), dma((NY - 1,)), dma((2,)),
            dma((NZ,)), dma((NZ,)), dma((NZ, 2 * NX - 2)), dma((NZ, 2 * NX - 2)),
            dma((NZ, 2)), dma((NZ, 2)), dma((NZ, 2)), dma((NZ, 2)),
            dma((6,)), dma((6,)), dma((2, NX)), dma((2, NX)),
            dma((NZ - 1, 2)), dma((2, NZ, 2)),
        ],
        compiler_params=pltpu.CompilerParams(
            collective_id=0, has_side_effects=True, vmem_limit_bytes=62 * 1024 * 1024
        ),
        name="hyena_li",
    )(streams, taps, decay, residues, init_state, out_weight)


def solution(mesh):
    in_specs = (
        P(None, None, "ctx", "tp"),
        P(None, None, "tp"),
        P(None, "tp"),
        P(None, "tp"),
        P(None, None, "tp"),
        P("tp", None),
    )
    return jax.shard_map(
        per_device, mesh=mesh, in_specs=in_specs, out_specs=P(None, "ctx", "tp"), check_vma=False
    )
```

```python
import jax
import jax.numpy as jnp
from jax import lax
from jax.experimental import pallas as pl
from jax.experimental.pallas import tpu as pltpu
from jax.sharding import PartitionSpec as P

MESH = pl.DeviceIdType.MESH
F32 = jnp.float32
BF16 = jnp.bfloat16
BY_X = (2, 3)

PLAN = {
    'barrier': ('p0', 'd0', 'd1', 'p1', 'p2', 'p3'),
    'states': (),
    'sent': ('d2', 'd3', 'f0'),
    'ends': (),
    'total': ('f1',),
    'gated': ('r0',),
    'near': ('l2',),
    'far': ('f2', 'r1', 'l3'),
    'k1': ('f3',),
    'k2': (),
}

NX, NZ, NY, NH = 4, 4, 4, 2
SUB = 8
LANES = 128
HALO = 16


def order_of(z, k):
    if k == 0:
        return jnp.where(z < 2, 3, 0)
    if k == 1:
        return jnp.where(z == 0, 2, jnp.where(z == 1, 0, jnp.where(z == 2, 3, 1)))
    if k == 2:
        return jnp.where(z % 2 == 0, 1, 2)
    return z


def kernel(
    streams, taps, decay, residues, init, weight, out,
    xbf, halo, xs, q_s, d_s, r_s, tapb, decb, resb, lst, ent, ebuf, tbuf, own_e,
    w_own, w_far, gat, pbuf, sendbuf, rbuf, pfin,
    load_sem, wload_sem, halo_sem, e_ssem, e_rsem, t_sem,
    wp_ssem, wp_rsem, wd_ssem, wd_rsem, ready_sem, f1_ssem, f1_rsem, f2_ssem, f2_rsem,
    g_ssem, g_rsem, gp_ssem, gp_rsem, z_ssem, z_rsem,
):
    tp, ctx = lax.axis_index("tp"), lax.axis_index("ctx")
    core, x, z = tp % 2, (tp // 2) % NX, tp // (2 * NX)
    y, zh = ctx % NY, ctx // NY
    nctx = NY * NH
    length = streams.shape[2]
    chans = streams.shape[3]
    poles = decay.shape[0]
    tap_count = taps.shape[1]
    lag = tap_count - 1
    sub_len = length // SUB
    half = length // 2
    groups = chans // LANES
    quarter = chans // NY

    def tp_of(zi, xi, ci):
        return (zi * NX + xi) * 2 + ci

    def dev(tp_index=tp, ctx_index=ctx):
        return {"ctx": ctx_index, "tp": tp_index}

    def remote(src, dst, ssem, rsem, where):
        return pltpu.make_async_remote_copy(
            src_ref=src, dst_ref=dst, send_sem=ssem, recv_sem=rsem, device_id=where, device_id_type=MESH
        )

    def ctx_of(hi, yi):
        return hi * NY + yi

    partner = dev(tp_of(z, x, 1 - core))
    xp, xm = (x + 1) % NX, (x + NX - 1) % NX
    yp, ym = (y + 1) % NY, (y + NY - 1) % NY
    ctx_next, ctx_prev = (ctx + 1) % nctx, (ctx + nctx - 1) % nctx

    barrier = pltpu.get_barrier_semaphore()

    def signal(where, sem=barrier):
        pl.semaphore_signal(sem, inc=1, device_id=where, device_id_type=MESH)

    greeted = [partner]
    for dx in range(1, NX):
        for dc in range(2):
            greeted.append(dev(tp_of(z, (x + dx) % NX, (core + dc) % 2)))
    for dy in range(1, NY):
        greeted.append(dev(tp, ctx_of(zh, (y + dy) % NY)))
    last_low = jnp.logical_and(zh == 0, y == NY - 1)
    first_high = jnp.logical_and(zh == 1, y == 0)

    @pl.when(first_high)
    def _():
        signal(dev(tp, ctx_prev))

    for where in greeted:
        signal(where)

    @pl.when(z > 0)
    def _():
        signal(dev(tp_of(z - 1, x, core)))

    @pl.when(z < NZ - 1)
    def _():
        signal(dev(tp_of(z + 1, x, core)))

    inner = jnp.where(z == 0, 1, jnp.where(z == NZ - 1, 1, 2))
    across = dev(tp, ctx_of(1 - zh, y))
    sent, awaited = [], []

    def go(copy):
        copy.start()
        sent.append(copy)

    def got(copy):
        copy.wait_recv()
        awaited.append(copy)

    load = pltpu.make_async_copy(streams.at[:, 0], xbf, load_sem)
    load.start()

    def w_cols(zt, xi, ci):
        return pl.ds(pl.multiple_of(tp_of(zt, xi, ci) * chans, chans), chans)

    own_loads = []
    for k in range(NZ):
        zt = order_of(z, k)
        own_loads.append(
            pltpu.make_async_copy(weight.at[:, w_cols(zt, x, core)], w_own.at[k, pl.ds(0, chans)], wload_sem.at[k])
        )
    load.wait()

    for g in range(groups):
        lanes = slice(g * LANES, (g + 1) * LANES)
        for s in range(3):
            for i in range(tap_count):
                tapb[g, s * tap_count + i] = jnp.broadcast_to(taps[s, i : i + 1, lanes], (SUB, LANES))
        for n in range(poles):
            decb[g, n] = jnp.broadcast_to(decay[n : n + 1, lanes], (SUB, LANES))
            resb[g, n] = jnp.broadcast_to(residues[n : n + 1, lanes], (SUB, LANES))
        for s in range(3):
            xs[s * groups + g, pl.ds(HALO, length), :] = xbf[s, :, lanes].astype(F32)

    def featurize(first, last):
        for g in range(groups):
            def one(j, carry, g=g):
                feats = []
                for s in range(3):
                    total = None
                    for i in range(tap_count):
                        rows = xs[s * groups + g, pl.ds(HALO + j - i, SUB, stride=sub_len), :]
                        term = tapb[g, s * tap_count + i] * rows
                        total = term if total is None else total + term
                    feats.append(total)
                q_s[g, j] = feats[0]
                d_s[g, j] = feats[1] * feats[2]
                return carry

            lax.fori_loop(first, last, one, 0, unroll=2)

    featurize(lag, sub_len)

    pl.semaphore_wait(barrier, len(greeted) + inner + jnp.where(last_low, 1, jnp.where(first_high, 2, zh)))

    @pl.when(zh == 0)
    def _():
        signal(across)

    @pl.when(last_low)
    def _():
        signal(dev(tp, ctx_next))

    @pl.when(zh == 1)
    def _():
        signal(across, ready_sem)


    halo_copy = remote(
        streams.at[:, 0, pl.ds(length - HALO, HALO)], halo, halo_sem.at[0], halo_sem.at[1], dev(tp, ctx_next)
    )

    @pl.when(ctx < nctx - 1)
    def _():
        halo_copy.start()

    wp_copies = [
        remote(
            weight.at[:, w_cols(order_of(z, k), x, 1 - core)],
            w_own.at[k, pl.ds(chans, chans)], wp_ssem.at[k], wp_rsem.at[k], partner,
        )
        for k in range(NZ)
    ]

    def own_rows(k):
        own_loads[k].start()
        go(wp_copies[k])

    def direct(k, q, kind):
        rows = pl.ds(pl.multiple_of(q * quarter, quarter), quarter)
        sends = []
        for dx in (1, 3, 2):
            for dc in range(2):
                xi, ci = (x + dx) % NX, (core + dc) % 2
                slot = (NX - dx) * 2 + dc - 2
                copy = remote(
                    weight.at[rows, w_cols(order_of(z, k), xi, ci)],
                    w_far.at[k, q, pl.ds(slot * quarter, quarter)],
                    wd_ssem.at[kind, k, slot], wd_rsem.at[kind, k, slot], dev(tp_of(z, xi, ci)),
                )
                sends.append(copy)
        return sends

    wd_copies = [direct(k, y, 0) for k in range(NZ)]
    late = {k: direct(k, (y + 2) % NY, 1) for k in BY_X}

    far_rows = w_far.shape[2]
    y_next, y_prev = dev(tp, ctx_of(zh, yp)), dev(tp, ctx_of(zh, ym))
    f1 = [
        [
            remote(w_far.at[k, y], w_far.at[k, y], f1_ssem.at[k, d], f1_rsem.at[k, d], where)
            for d, where in enumerate((y_next, y_prev))
        ]
        for k in range(NZ)
    ]
    top, bottom = pl.ds(0, far_rows // 2), pl.ds(far_rows // 2, far_rows // 2)
    f2 = [
        []
        if k in BY_X
        else [
            remote(w_far.at[k, ym, top], w_far.at[k, ym, top], f2_ssem.at[k, 0], f2_rsem.at[k, 0], y_next),
            remote(w_far.at[k, yp, bottom], w_far.at[k, yp, bottom], f2_ssem.at[k, 1], f2_rsem.at[k, 1], y_prev),
        ]
        for k in range(NZ)
    ]

    def act(kind, k):
        if kind == "p":
            own_rows(k)
        if kind == "d":
            for copy in wd_copies[k]:
                go(copy)
        if kind == "l":
            for copy in late[k]:
                go(copy)
        if kind == "f":
            for copy in wd_copies[k]:
                got(copy)
            for copy in f1[k]:
                go(copy)
        if kind == "r":
            for copy in f1[k]:
                got(copy)
            for copy in f2[k]:
                go(copy)

    def point(name):
        for step in PLAN[name]:
            act(step[0], int(step[1]))

    point("barrier")

    @pl.when(ctx > 0)
    def _():
        halo_copy.wait_recv()
        for g in range(groups):
            for s in range(3):
                xs[s * groups + g, pl.ds(0, HALO), :] = halo[s, :, g * LANES : (g + 1) * LANES].astype(F32)

    @pl.when(ctx == 0)
    def _():
        for g in range(groups):
            for s in range(3):
                xs[s * groups + g, pl.ds(0, HALO), :] = jnp.zeros((HALO, LANES), F32)

    featurize(0, lag)

    point("states")

    for g in range(groups):
        def step(j, states, g=g):
            driven = d_s[g, j]
            new = tuple(decb[g, n] * states[n] + driven for n in range(poles))
            parts = [resb[g, n] * new[n] for n in range(poles)]
            while len(parts) > 1:
                parts = [a + b for a, b in zip(parts[::2], parts[1::2])]
            r_s[g, j] = parts[0]
            return new

        states = lax.fori_loop(0, sub_len, step, tuple(jnp.zeros((SUB, LANES), F32) for _ in range(poles)), unroll=2)
        for n in range(poles):
            lst[g, pl.ds(n * SUB, SUB), :] = states[n]

    def power(value, count):
        result, base = None, value
        while count:
            if count % 2:
                result = base if result is None else result * base
            count //= 2
            if count:
                base = base * base
        return result

    for g in range(groups):
        lanes = slice(g * LANES, (g + 1) * LANES)
        sub_decay = power(decay[:, lanes], sub_len)
        running = jnp.zeros((poles, LANES), F32)
        for s in range(SUB):
            ent[g, s] = running
            running = sub_decay * running + lst[g, pl.ds(s, poles, stride=SUB), :]
        own_e[:, lanes] = running

    e_copies = [
        remote(own_e, ebuf.at[dy - 1], e_ssem.at[dy - 1], e_rsem.at[dy - 1], dev(tp, ctx_of(zh, (y + dy) % NY)))
        for dy in range(1, NY)
    ]
    for copy in e_copies:
        go(copy)

    point("sent")

    for copy in e_copies:
        got(copy)

    point("ends")

    def select_power(powers, exponent):
        value = jnp.broadcast_to(jnp.where(exponent == 0, F32(1.0), F32(0.0)), powers[0].shape)
        for e, p in enumerate(powers):
            value = jnp.where(exponent == e + 1, p, value)
        return value

    t_copy = remote(tbuf.at[0], tbuf.at[1], t_sem.at[0], t_sem.at[1], dev(tp, ctx_of(1 - zh, y)))

    shard_decay = power(decay[...], length)
    powers = [shard_decay, shard_decay * shard_decay]
    powers.append(powers[1] * shard_decay)

    @pl.when(zh == 0)
    def _():
        total = powers[2] * shard_decay * init[0] + select_power(powers, 3 - y) * own_e[...]
        for dy in range(1, NY):
            total = total + select_power(powers, 3 - (y + NY - dy) % NY) * ebuf[dy - 1]
        tbuf[0] = total
        pl.semaphore_wait(ready_sem, 1)
        t_copy.start()
        tbuf[2] = init[0]

    @pl.when(zh == 1)
    def _():
        t_copy.wait_recv()
        tbuf[2] = tbuf[1]

    incoming = select_power(powers, y) * tbuf[2]
    for dy in range(1, NY):
        gain = F32(1.0) if dy == 1 else powers[dy - 2]
        incoming = incoming + jnp.where(y >= dy, gain * ebuf[dy - 1], F32(0.0))

    point("total")

    for g in range(groups):
        lanes = slice(g * LANES, (g + 1) * LANES)
        sub_decay = power(decay[:, lanes], sub_len)
        arriving = incoming[:, lanes]
        for s in range(SUB):
            lst[g, pl.ds(s, poles, stride=SUB), :] = (ent[g, s] + arriving) * residues[:, lanes]
            arriving = arriving * sub_decay

    for g in range(groups):
        states = tuple(lst[g, pl.ds(n * SUB, SUB), :] for n in range(poles))
        for h in range(2):
            def pair(jj, states, g=g, h=h):
                rows = []
                for b in range(2):
                    j = h * (sub_len // 2) + 2 * jj + b
                    states = tuple(decb[g, n] * states[n] for n in range(poles))
                    parts = list(states)
                    while len(parts) > 1:
                        parts = [u + v for u, v in zip(parts[::2], parts[1::2])]
                    rows.append(q_s[g, j] * (r_s[g, j] + parts[0]))
                at = pl.ds(pl.multiple_of(jj * 2 * SUB, 2 * SUB), 2 * SUB)
                gat[h, at, g * LANES : (g + 1) * LANES] = jnp.concatenate(rows, axis=0).astype(BF16)
                return states

            states = lax.fori_loop(0, sub_len // 4, pair, states)

    def block(h, slot):
        return gat.at[h, :, pl.ds(slot * chans, chans)]

    def g_copy(h, src_slot, dst_slot, at, where):
        return remote(block(h, src_slot), block(h, dst_slot), g_ssem.at[at], g_rsem.at[at], where)

    def p_copy(h, slot):
        return remote(
            block(h, slot), block(h, slot + 1), gp_ssem.at[h, slot // 2], gp_rsem.at[h, slot // 2], partner
        )

    to_right, to_left = dev(tp_of(z, xp, core)), dev(tp_of(z, xm, core))
    right = [g_copy(0, 0, 6, 0, to_right), g_copy(1, 0, 6, 1, to_right)]
    left = [g_copy(0, 0, 2, 2, to_left), g_copy(1, 0, 2, 3, to_left)]
    relay_right = g_copy(0, 6, 4, 4, to_right)
    relay_left = g_copy(1, 2, 4, 5, to_left)
    go(right[0])
    go(left[1])
    go(right[1])
    go(left[0])
    p_copies = [[p_copy(h, slot) for slot in (0, 2, 4, 6)] for h in range(2)]
    for h in range(2):
        go(p_copies[h][0])

    point("gated")
    got(right[0])
    go(relay_right)
    go(p_copies[0][3])
    got(left[1])
    go(relay_left)
    go(p_copies[1][1])
    got(right[1])
    go(p_copies[1][3])
    got(left[0])
    go(p_copies[0][1])
    point("near")
    got(relay_right)
    go(p_copies[0][2])
    got(relay_left)
    go(p_copies[1][2])
    point("far")
    for h in range(2):
        for copy in p_copies[h]:
            got(copy)

    for k in range(NZ):
        if k in (1, 2):
            point("k1" if k == 1 else "k2")
        zt = order_of(z, k)
        own_loads[k].wait()
        got(wp_copies[k])
        if k in BY_X:
            for copy in f1[k] + late[k]:
                got(copy)
        for copy in f2[k]:
            got(copy)
        pieces = [w_own[k]]
        for slot in range(2 * NX - 2):
            for q in range(NY):
                pieces.append(w_far[k, q, slot * quarter : (slot + 1) * quarter])
        w_all = jnp.concatenate(pieces, axis=0)
        for h in range(2):
            product = jnp.dot(gat[h], w_all, preferred_element_type=F32)
            if k < NZ - 1:
                heading = jnp.where(zt > z, 0, 1)
                target = jnp.where(zt > z, z + 1, z - 1)
                copy = remote(
                    sendbuf.at[k, h], rbuf.at[heading, zt, h], z_ssem.at[k, h], z_rsem.at[heading, zt, h],
                    dev(tp_of(target, x, core)),
                )
                pbuf[...] = product
                has_in = jnp.where(zt > z, z > 0, z < NZ - 1)

                @pl.when(has_in)
                def _(copy=copy, heading=heading, zt=zt, h=h):
                    got(copy)
                    pbuf[...] += rbuf[heading, zt, h].astype(F32)

                sendbuf[k, h] = pbuf[...].astype(BF16)
                go(copy)
            else:
                pbuf[...] = product

                @pl.when(z > 0)
                def _(h=h):
                    remote(
                        sendbuf.at[0, h], rbuf.at[0, z, h], z_ssem.at[0, h], z_rsem.at[0, z, h], partner
                    ).wait_recv()
                    pbuf[...] += rbuf[0, z, h].astype(F32)

                @pl.when(z < NZ - 1)
                def _(h=h):
                    remote(
                        sendbuf.at[0, h], rbuf.at[1, z, h], z_ssem.at[0, h], z_rsem.at[1, z, h], partner
                    ).wait_recv()
                    pbuf[...] += rbuf[1, z, h].astype(F32)

                for g in range(groups):
                    pfin[g, pl.ds(h * half, half), :] = pbuf[:, g * LANES : (g + 1) * LANES]

    for g in range(groups):
        for s in range(SUB):
            out[0, s * sub_len : (s + 1) * sub_len, g * LANES : (g + 1) * LANES] = pfin[
                g, pl.ds(s, sub_len, stride=SUB), :
            ].astype(BF16)

    @pl.when(ctx < nctx - 1)
    def _():
        halo_copy.wait_send()

    @pl.when(zh == 0)
    def _():
        t_copy.wait_send()

    for copy in sent:
        copy.wait_send()


def per_device(streams, taps, decay, residues, init_state, out_weight):
    length, chans = streams.shape[2], streams.shape[3]
    poles, tap_count = decay.shape[0], taps.shape[1]
    groups, sub_len, half, quarter = chans // LANES, length // SUB, length // 2, chans // NY
    vmem = pl.BlockSpec(memory_space=pltpu.VMEM)
    hbm = pl.BlockSpec(memory_space=pl.ANY)
    dma = pltpu.SemaphoreType.DMA
    return pl.pallas_call(
        kernel,
        out_shape=jax.ShapeDtypeStruct((1, length, chans), BF16),
        in_specs=[hbm, vmem, vmem, vmem, vmem, hbm],
        out_specs=vmem,
        scratch_shapes=[
            pltpu.VMEM((3, length, chans), BF16),
            pltpu.VMEM((3, HALO, chans), BF16),
            pltpu.VMEM((3 * groups, HALO + length, LANES), F32),
            pltpu.VMEM((groups, sub_len, SUB, LANES), F32),
            pltpu.VMEM((groups, sub_len, SUB, LANES), F32),
            pltpu.VMEM((groups, sub_len, SUB, LANES), F32),
            pltpu.VMEM((groups, 3 * tap_count, SUB, LANES), F32),
            pltpu.VMEM((groups, poles, SUB, LANES), F32),
            pltpu.VMEM((groups, poles, SUB, LANES), F32),
            pltpu.VMEM((groups, poles * SUB, LANES), F32),
            pltpu.VMEM((groups, SUB, poles, LANES), F32),
            pltpu.VMEM((NY - 1, poles, chans), F32),
            pltpu.VMEM((3, poles, chans), F32),
            pltpu.VMEM((poles, chans), F32),
            pltpu.VMEM((NZ, 2 * chans, chans), BF16),
            pltpu.VMEM((NZ, NY, (2 * NX - 2) * quarter, chans), BF16),
            pltpu.VMEM((2, half, 2 * NX * chans), BF16),
            pltpu.VMEM((half, chans), F32),
            pltpu.VMEM((NZ - 1, 2, half, chans), BF16),
            pltpu.VMEM((2, NZ, 2, half, chans), BF16),
            pltpu.VMEM((groups, length, LANES), F32),
            dma(()), dma((NZ,)), dma((2,)), dma((NY - 1,)), dma((NY - 1,)), dma((2,)),
            dma((NZ,)), dma((NZ,)), dma((2, NZ, 2 * NX - 2)), dma((2, NZ, 2 * NX - 2)), pltpu.SemaphoreType.REGULAR,
            dma((NZ, 2)), dma((NZ, 2)), dma((NZ, 2)), dma((NZ, 2)),
            dma((6,)), dma((6,)), dma((2, NX)), dma((2, NX)),
            dma((NZ - 1, 2)), dma((2, NZ, 2)),
        ],
        compiler_params=pltpu.CompilerParams(
            collective_id=0, has_side_effects=True, vmem_limit_bytes=62 * 1024 * 1024
        ),
        name="hyena_li",
    )(streams, taps, decay, residues, init_state, out_weight)


def solution(mesh):
    in_specs = (
        P(None, None, "ctx", "tp"),
        P(None, None, "tp"),
        P(None, "tp"),
        P(None, "tp"),
        P(None, None, "tp"),
        P("tp", None),
    )
    return jax.shard_map(
        per_device, mesh=mesh, in_specs=in_specs, out_specs=P(None, "ctx", "tp"), check_vma=False
    )
```
